32 devices in a mesh: seq: 2 (over x), hist: 8 (over z, y), chan: 2 (over core).
Axes of the slice: x: 2, y: 2, z: 4, core: 2. Of those that a mesh axis runs over, the one named last changes fastest.
Arguments:
- history: bfloat16 [4096, 4096], P(('seq', 'hist'), 'chan'), parts along dimension 0, may hold values from -6 to 6
- filter_taps: bfloat16 [2048, 4096], P('hist', 'chan'), may hold values from -0.125 to 0.125
- gate_values: bfloat16 [512, 4096], P(('seq', 'hist'), 'chan'), parts along dimension 0, may hold values from -6 to 6
- out_weight: bfloat16 [4096, 4096], P('chan', 'hist'), may hold values from -0.09375 to 0.09375
Outputs:
- output: bfloat16 [512, 4096], P(('seq', 'hist', 'chan')), parts along dimension 0
The draws below stay inside these ranges and needn't reach their ends.
There are 2 independent parts, one for each index of `seq`. The reference program is written for one: setup_inputs(seed, part) draws one part's arguments, and reference() takes and returns one part's arrays. A program takes and returns all parts, laid end to end along the dimension named above; an argument that names none is the same for every part. Nothing has to cross between parts.
All inputs are finite; a program needn't handle non-finite values.
Results may differ from the reference program's by a relative error of at most 0.013.
Values may be sent and summed in bfloat16 or wider, within the bound.
A program may use at most 64 MiB of HBM per device.

```python
import jax
import jax.numpy as jnp
from jax import lax

D = 4096
TB = 256
HIST = 2048


def level_of(own_key, shape, split, low, largest):
    factor_of = 1.0
    for dim, parts in split:
        steps = jax.random.uniform(jax.random.fold_in(jax.random.fold_in(own_key, 6), dim), (parts,), jnp.float32, low / len(split), largest / len(split))
        factor_of = factor_of * jnp.repeat(jnp.exp(steps), shape[dim] // parts).reshape((-1,) + (1,) * (len(shape) - 1 - dim))
    return factor_of


def centred(rng, extent, width, bound, pieces=(), dtype=jnp.bfloat16):
    values = jax.random.normal(rng, extent, jnp.float32) * width
    if len(pieces) > 0:
        values = level_of(rng, extent, pieces, -0.22, 0.18) * values
    return jnp.clip(values, min=-bound, max=bound).astype(dtype)


def setup_inputs(seed: int = 0, part: int = 0) -> dict:
    keys = jax.random.split(jax.random.key(seed), 5)
    part_keys = jax.random.split(jax.random.fold_in(keys[4], part), 5)
    history = centred(part_keys[0], (HIST, D), 1.0, 6.0, ((0, 8), (1, 2)))
    filter_taps = centred(keys[1], (HIST, D), (HIST ** -0.5), 0.125, ((0, 8), (1, 2)))
    gate_values = centred(part_keys[2], (TB, D), 1.0, 6.0, ((0, 8), (1, 2)))
    out_weight = centred(keys[3], (D, D), D ** -0.5, 0.09375, ((0, 2), (1, 8)))
    return dict(history=history, filter_taps=filter_taps, gate_values=gate_values, out_weight=out_weight)


def reference(history, filter_taps, gate_values, out_weight):
    block_width = min(256, D)
    count_blocks = D // block_width
    signal = history.astype(jnp.float32).reshape(HIST, count_blocks, block_width).transpose(1, 0, 2)
    kernel = filter_taps.astype(jnp.float32)[::-1].reshape(HIST, count_blocks, block_width).transpose(1, 0, 2)
    length = 2 * HIST

    def conv_block(pair):
        inputs, taps_block = pair
        spectrum = jnp.fft.rfft(inputs, length, axis=0) * jnp.fft.rfft(taps_block, length, axis=0)
        whole = jnp.fft.irfft(spectrum, length, axis=0)
        return whole[HIST - TB:HIST]

    blocks = lax.map(conv_block, (signal, kernel))
    conv = blocks.transpose(1, 0, 2).reshape(TB, D).astype(jnp.float32)
    gated = (conv * gate_values.astype(jnp.float32)).astype(jnp.bfloat16)
    return jnp.dot(gated, out_weight, preferred_element_type=jnp.float32).astype(jnp.bfloat16)
```

```python
import functools
import math

import jax
import jax.numpy as jnp
import numpy as np
from jax import lax
from jax.experimental import pallas as pl
from jax.experimental.pallas import tpu as pltpu
from jax.sharding import PartitionSpec as P

MESH = pl.DeviceIdType.MESH
BF16 = jnp.bfloat16
F32 = jnp.float32
CHUNKS = 4


def tables(local_rows, block_tokens):
    period = local_rows + block_tokens
    modes = period // 2
    odd = 2 * np.arange(modes) + 1
    turn = math.pi / period
    places = np.arange(period)
    phase = (np.outer(odd, places) % (2 * period)) * turn
    forward = np.concatenate([np.cos(phase), np.sin(phase)], 0)
    lags = block_tokens - 1 - np.arange(block_tokens)
    phase = (np.outer(lags, odd) % (2 * period)) * turn
    inverse = np.concatenate([np.cos(phase), -np.sin(phase)], 1) * (2.0 / period)
    return forward, inverse


def spectrum_product(taps, values):
    half = taps.shape[0] // 2
    tc, ts, vc, vs = taps[:half], taps[half:], values[:half], values[half:]
    return tc * vc + ts * vs, tc * vs - ts * vc


def dot(a, b):
    return jnp.dot(a, b, preferred_element_type=F32)


def local_general(history, filter_taps, gate_values, out_weight):
    local_rows, channels = history.shape
    owned_rows = gate_values.shape[0]
    count_hist = lax.axis_size("hist")
    count_chan = lax.axis_size("chan")
    block_tokens = owned_rows * count_hist
    forward, inverse = tables(local_rows, block_tokens)
    forward = jnp.asarray(forward, F32)
    forward_high = forward.astype(BF16)
    forward_low = (forward - forward_high.astype(F32)).astype(BF16)
    inverse = jnp.asarray(inverse, F32)
    next_taps = lax.ppermute(
        filter_taps, "hist", [(source, source - 1) for source in range(1, count_hist)]
    )
    extended = jnp.concatenate([filter_taps, next_taps], 0)[: forward.shape[1]]
    spec_taps = dot(forward_high, extended) + dot(forward_low, extended)
    spec_input = dot(forward_high[:, :local_rows], history) + dot(
        forward_low[:, :local_rows], history
    )
    spectrum = jnp.concatenate(spectrum_product(spec_taps, spec_input), 0)
    partial_conv = jnp.dot(
        inverse, spectrum, precision=lax.Precision.HIGHEST, preferred_element_type=F32
    )
    conv = lax.psum_scatter(partial_conv, "hist", scatter_dimension=0, tiled=True)
    gated = (conv * gate_values.astype(F32)).astype(BF16)
    partial_value = dot(lax.all_gather(gated, "hist", axis=0, tiled=True), out_weight)
    columns = partial_value.shape[1]
    half_rows = owned_rows // count_chan
    ordered = partial_value.reshape(count_hist, count_chan, half_rows, columns)
    ordered = ordered.transpose(1, 0, 2, 3).reshape(-1, columns)
    summed = lax.psum_scatter(ordered.astype(BF16), "chan", scatter_dimension=0, tiled=True)
    return lax.all_to_all(summed, "hist", split_axis=0, concat_axis=1, tiled=True)


def kernel(
    pairs, chunks, hist_ref, taps_ref, gate_ref, weight_ref, fwd_ref, inv_ref, out_ref,
    taps_buf, hist_buf, gate_buf, weight_buf, fwd_buf, inv_buf,
    send_buf, own_buf, recv_buf, gated_buf, acc_buf, swap_send, swap_recv, fin_buf, res_buf,
    load_sem, own_sem, xt_send, xt_recv, xh_send, xh_recv, xg_send, xg_recv,
    zt_send, zt_recv, rs_send, rs_recv, az_send, az_recv, ay_send, ay_recv,
    sw_send, sw_recv, fin_send, fin_recv,
):
    me = lax.axis_index("hist")
    core = lax.axis_index("chan")
    p = me // 2
    q = me % 2
    total = 2 * pairs
    rows = hist_ref.shape[0]
    half = hist_ref.shape[1] // 2
    width = half // chunks
    columns = weight_ref.shape[1]
    partner = 2 * p + (1 - q)
    modes = fwd_buf.shape[0] // 2

    def remote(src, dst, send, recv, where):
        return pltpu.make_async_remote_copy(
            src_ref=src, dst_ref=dst, send_sem=send, recv_sem=recv,
            device_id=where, device_id_type=MESH,
        )

    def cols(side, ch):
        return pl.ds(pl.multiple_of(side * half + ch * width, width), width)

    barrier = pltpu.get_barrier_semaphore()
    for d in range(1, total):
        pl.semaphore_signal(
            barrier, inc=1, device_id={"hist": (me + d) % total}, device_id_type=MESH
        )
    pl.semaphore_signal(barrier, inc=1, device_id={"chan": 1 - core}, device_id_type=MESH)

    own = []
    for ch in range(chunks):
        own.append((
            pltpu.make_async_copy(taps_ref.at[:, cols(q, ch)], taps_buf.at[q, ch], own_sem.at[0, ch]),
            pltpu.make_async_copy(hist_ref.at[:, cols(q, ch)], hist_buf.at[q, ch], own_sem.at[1, ch]),
        ))
        for copy in own[-1]:
            copy.start()
    gate_side = pl.ds(pl.multiple_of(q * half, half), half)
    gate_other = pl.ds(pl.multiple_of((1 - q) * half, half), half)
    loads = [
        pltpu.make_async_copy(fwd_ref, fwd_buf, load_sem.at[0]),
        pltpu.make_async_copy(inv_ref, inv_buf, load_sem.at[1]),
        pltpu.make_async_copy(gate_ref.at[:, gate_side], gate_buf.at[q], load_sem.at[2]),
        pltpu.make_async_copy(weight_ref, weight_buf, load_sem.at[3]),
    ]
    for copy in loads:
        copy.start()

    @pl.when(p == pairs - 1)
    def _():
        taps_buf[2] = jnp.zeros(taps_buf.shape[1:], BF16)

    pl.semaphore_wait(barrier, total)

    xt, xh, zt = [], [], []
    for ch in range(chunks):
        xt.append(remote(taps_ref.at[:, cols(1 - q, ch)], taps_buf.at[q, ch],
                         xt_send.at[ch], xt_recv.at[ch], {"hist": partner}))
        xt[-1].start()
    for ch in range(chunks):
        xh.append(remote(hist_ref.at[:, cols(1 - q, ch)], hist_buf.at[q, ch],
                         xh_send.at[ch], xh_recv.at[ch], {"hist": partner}))
        xh[-1].start()
        if ch == 0:
            xg = remote(gate_ref.at[:, gate_other], gate_buf.at[q], xg_send, xg_recv,
                        {"hist": partner})
            xg.start()
    for ch in range(chunks):
        zt.append(remote(taps_buf.at[0, ch], taps_buf.at[2, ch], zt_send.at[ch], zt_recv.at[ch],
                         {"hist": jnp.maximum(me - 2, 0)}))
    for ch in range(chunks):
        own[ch][0].wait()

        @pl.when((q == 0) & (p > 0))
        def _():
            zt[ch].start()

    for ch in range(chunks):
        xt[ch].wait_recv()

        @pl.when((q == 1) & (p > 0))
        def _():
            zt[ch].start()

    loads[0].wait()
    loads[1].wait()

    rs, az, ay = {}, {}, {}

    def compute(ch):
        own[ch][1].wait()

        @pl.when(p < pairs - 1)
        def _():
            zt[ch].wait_recv()

        t0, t1, t2 = (taps_buf[i, ch] for i in range(3))
        first = fwd_buf[:, :rows]
        second = fwd_buf[:, rows:]
        s_a = dot(first, t0) + dot(second, t1)
        s_b = dot(first, t1) + dot(second, t2)
        xh[ch].wait_recv()
        h_a = dot(first, hist_buf[0, ch])
        h_b = dot(first, hist_buf[1, ch])
        ra, ia = spectrum_product(s_a, h_a)
        rb, ib = spectrum_product(s_b, h_b)
        conv = dot(inv_buf[:, :modes], (ra + rb).astype(BF16)) + dot(
            inv_buf[:, modes:], (ia + ib).astype(BF16)
        )
        conv = conv.reshape(pairs, conv.shape[0] // pairs, width)
        send_buf[ch] = conv.astype(BF16)
        own_buf[ch] = conv
        for d in range(1, pairs):
            to = (p + d) % pairs
            rs[ch, d] = remote(send_buf.at[ch, to], recv_buf.at[ch, d - 1],
                               rs_send.at[ch, d - 1], rs_recv.at[ch, d - 1],
                               {"hist": 2 * to + q})
            rs[ch, d].start()

    def reduce(ch):
        if ch == 0:
            loads[2].wait()
            xg.wait_recv()
        value = own_buf[ch, p]
        for d in range(1, pairs):
            rs[ch, d].wait_recv()
            value = value + recv_buf[ch, d - 1].astype(F32)
        gates = gate_buf[:, :, ch * width:(ch + 1) * width].astype(F32)
        gated = (value * gates.reshape(value.shape)).astype(BF16)
        gated_buf[ch, q, p] = gated
        slot = gated_buf.at[ch, q, p]
        for d in range(1, pairs):
            az[ch, d] = remote(slot, slot, az_send.at[ch, d - 1], az_recv.at[ch, d - 1],
                               {"hist": 2 * ((p + d) % pairs) + q})
            az[ch, d].start()
        ay[ch, 0] = remote(slot, slot, ay_send.at[ch, 0], ay_recv.at[ch, 0], {"hist": partner})
        ay[ch, 0].start()

    def forward(ch):
        for d in range(1, pairs):
            az[ch, d].wait_recv()
            slot = gated_buf.at[ch, q, (p - d + pairs) % pairs]
            ay[ch, d] = remote(slot, slot, ay_send.at[ch, d], ay_recv.at[ch, d], {"hist": partner})
            ay[ch, d].start()

    def project(ch):
        if ch == 0:
            loads[3].wait()
        for d in range(pairs):
            ay[ch, d].wait_recv()
        low = gated_buf[ch, 0].reshape(-1, width)
        high = gated_buf[ch, 1].reshape(-1, width)
        value = dot(low, weight_buf[ch * width:(ch + 1) * width]) + dot(
            high, weight_buf[half + ch * width:half + (ch + 1) * width]
        )
        value = value.reshape(acc_buf.shape)
        if ch == 0:
            acc_buf[...] = value
        else:
            acc_buf[...] += value

    for step in range(chunks + 3):
        if step < chunks:
            compute(step)
        if 0 <= step - 1 < chunks:
            reduce(step - 1)
        if 0 <= step - 2 < chunks:
            forward(step - 2)
        if 0 <= step - 3 < chunks:
            project(step - 3)

    swap_send[...] = acc_buf[:, 1 - core].astype(BF16)
    swap = remote(swap_send, swap_recv, sw_send, sw_recv, {"chan": 1 - core})
    swap.start()
    swap.wait_recv()
    fin_buf[...] = (acc_buf[:, core] + swap_recv[...].astype(F32)).astype(BF16)
    fin = []
    for d in range(1, total):
        to = (me + d) % total
        fin.append(remote(fin_buf.at[to], res_buf.at[me], fin_send.at[d - 1], fin_recv.at[d - 1],
                          {"hist": to}))
        fin[-1].start()
    res_buf[me] = fin_buf[me]

    for ch in range(chunks):
        xt[ch].wait_send()
        xh[ch].wait_send()

        @pl.when(p > 0)
        def _():
            zt[ch].wait_send()

    xg.wait_send()
    for group in (rs, az, ay):
        for copy in group.values():
            copy.wait_send()
    swap.wait_send()
    for copy in fin:
        copy.wait_recv()
    for k in range(total):
        out_ref[:, k * columns:(k + 1) * columns] = res_buf[k]
    for copy in fin:
        copy.wait_send()


def local_kernel(chunks, history, filter_taps, gate_values, out_weight):
    rows, channels = history.shape
    owned = gate_values.shape[0]
    total = lax.axis_size("hist")
    cores = lax.axis_size("chan")
    pairs = total // 2
    tokens = owned * total
    half = channels // 2
    width = half // chunks
    columns = out_weight.shape[1]
    part = owned // cores
    forward, inverse = tables(rows, tokens)
    modes2 = forward.shape[0]
    forward = jnp.asarray(forward, F32).astype(BF16)
    inverse = jnp.asarray(inverse, F32).astype(BF16)
    dma = pltpu.SemaphoreType.DMA
    others = pairs - 1
    scratch = [
        pltpu.VMEM((3, chunks, rows, width), BF16),
        pltpu.VMEM((2, chunks, rows, width), BF16),
        pltpu.VMEM((2, owned, half), BF16),
        pltpu.VMEM(out_weight.shape, BF16),
        pltpu.VMEM(forward.shape, BF16),
        pltpu.VMEM(inverse.shape, BF16),
        pltpu.VMEM((chunks, pairs, 2 * owned, width), BF16),
        pltpu.VMEM((chunks, pairs, 2 * owned, width), F32),
        pltpu.VMEM((chunks, others, 2 * owned, width), BF16),
        pltpu.VMEM((chunks, 2, pairs, 2 * owned, width), BF16),
        pltpu.VMEM((total, cores, part, columns), F32),
        pltpu.VMEM((total, part, columns), BF16),
        pltpu.VMEM((total, part, columns), BF16),
        pltpu.VMEM((total, part, columns), BF16),
        pltpu.VMEM((total, part, columns), BF16),
        dma((4,)), dma((2, chunks)),
        dma((chunks,)), dma((chunks,)), dma((chunks,)), dma((chunks,)), dma, dma,
        dma((chunks,)), dma((chunks,)),
        dma((chunks, others)), dma((chunks, others)),
        dma((chunks, others)), dma((chunks, others)),
        dma((chunks, pairs)), dma((chunks, pairs)),
        dma, dma, dma((total - 1,)), dma((total - 1,)),
    ]
    return pl.pallas_call(
        functools.partial(kernel, pairs, chunks),
        out_shape=jax.ShapeDtypeStruct((part, total * columns), BF16),
        in_specs=[pl.BlockSpec(memory_space=pl.ANY)] * 6,
        out_specs=pl.BlockSpec(memory_space=pltpu.VMEM),
        scratch_shapes=scratch,
        compiler_params=pltpu.CompilerParams(
            collective_id=0, has_side_effects=True, vmem_limit_bytes=32 * 1024 * 1024
        ),
    )(history, filter_taps, gate_values, out_weight, forward, inverse)


def local(history, filter_taps, gate_values, out_weight):
    rows, channels = history.shape
    owned = gate_values.shape[0]
    total = lax.axis_size("hist")
    cores = lax.axis_size("chan")
    fits = (
        total % 2 == 0
        and total >= 4
        and cores == 2
        and owned % (16 * cores) == 0
        and rows == owned * total
        and channels % (256 * CHUNKS) == 0
        and out_weight.shape[1] % 128 == 0
    )
    if fits:
        return local_kernel(CHUNKS, history, filter_taps, gate_values, out_weight)
    return local_general(history, filter_taps, gate_values, out_weight)


def solution(mesh):
    return jax.shard_map(
        local,
        mesh=mesh,
        in_specs=(
            P(("seq", "hist"), "chan"),
            P("hist", "chan"),
            P(("seq", "hist"), "chan"),
            P("chan", "hist"),
        ),
        out_specs=P(("seq", "hist", "chan"), None),
        check_vma=False,
    )
```

```python
import functools
import math

import jax
import jax.numpy as jnp
import numpy as np
from jax import lax
from jax.experimental import pallas as pl
from jax.experimental.pallas import tpu as pltpu
from jax.sharding import PartitionSpec as P

MESH = pl.DeviceIdType.MESH
BF16 = jnp.bfloat16
F32 = jnp.float32
CHUNKS = 4


def tables(local_rows, block_tokens):
    period = local_rows + block_tokens
    modes = period // 2
    odd = 2 * np.arange(modes) + 1
    turn = math.pi / period
    places = np.arange(period)
    phase = (np.outer(odd, places) % (2 * period)) * turn
    forward = np.concatenate([np.cos(phase), np.sin(phase)], 0)
    lags = block_tokens - 1 - np.arange(block_tokens)
    phase = (np.outer(lags, odd) % (2 * period)) * turn
    inverse = np.concatenate([np.cos(phase), -np.sin(phase)], 1) * (2.0 / period)
    return forward, inverse


def spectrum_product(taps, values):
    half = taps.shape[0] // 2
    tc, ts, vc, vs = taps[:half], taps[half:], values[:half], values[half:]
    return tc * vc + ts * vs, tc * vs - ts * vc


def dot(a, b):
    return jnp.dot(a, b, preferred_element_type=F32)


def local_general(history, filter_taps, gate_values, out_weight):
    local_rows, channels = history.shape
    owned_rows = gate_values.shape[0]
    count_hist = lax.axis_size("hist")
    count_chan = lax.axis_size("chan")
    block_tokens = owned_rows * count_hist
    forward, inverse = tables(local_rows, block_tokens)
    forward = jnp.asarray(forward, F32)
    forward_high = forward.astype(BF16)
    forward_low = (forward - forward_high.astype(F32)).astype(BF16)
    inverse = jnp.asarray(inverse, F32)
    next_taps = lax.ppermute(
        filter_taps, "hist", [(source, source - 1) for source in range(1, count_hist)]
    )
    extended = jnp.concatenate([filter_taps, next_taps], 0)[: forward.shape[1]]
    spec_taps = dot(forward_high, extended) + dot(forward_low, extended)
    spec_input = dot(forward_high[:, :local_rows], history) + dot(
        forward_low[:, :local_rows], history
    )
    spectrum = jnp.concatenate(spectrum_product(spec_taps, spec_input), 0)
    partial_conv = jnp.dot(
        inverse, spectrum, precision=lax.Precision.HIGHEST, preferred_element_type=F32
    )
    conv = lax.psum_scatter(partial_conv, "hist", scatter_dimension=0, tiled=True)
    gated = (conv * gate_values.astype(F32)).astype(BF16)
    partial_value = dot(lax.all_gather(gated, "hist", axis=0, tiled=True), out_weight)
    columns = partial_value.shape[1]
    half_rows = owned_rows // count_chan
    ordered = partial_value.reshape(count_hist, count_chan, half_rows, columns)
    ordered = ordered.transpose(1, 0, 2, 3).reshape(-1, columns)
    summed = lax.psum_scatter(ordered.astype(BF16), "chan", scatter_dimension=0, tiled=True)
    return lax.all_to_all(summed, "hist", split_axis=0, concat_axis=1, tiled=True)


def kernel(
    pairs, chunks, hist_ref, taps_ref, gate_ref, weight_ref, fwd_ref, inv_ref, out_ref,
    taps_buf, hist_buf, gate_buf, weight_buf, fwd_buf, inv_buf,
    send_buf, own_buf, recv_buf, gated_buf, acc_buf, swap_send, swap_recv, fin_buf, res_buf,
    load_sem, own_sem, xt_send, xt_recv, xh_send, xh_recv, xg_send, xg_recv,
    zt_send, zt_recv, xf_send, xf_recv, xz_send, xz_recv, rs_send, rs_recv, az_send, az_recv, ay_send, ay_recv,
    sw_send, sw_recv, fin_send, fin_recv,
):
    me = lax.axis_index("hist")
    core = lax.axis_index("chan")
    seq = lax.axis_index("seq")
    p = me // 2
    q = me % 2
    total = 2 * pairs
    rows = hist_ref.shape[0]
    half = hist_ref.shape[1] // 2
    width = half // chunks
    columns = weight_ref.shape[1]
    partner = 2 * p + (1 - q)
    modes = fwd_buf.shape[0] // 2

    def remote(src, dst, send, recv, where):
        return pltpu.make_async_remote_copy(
            src_ref=src, dst_ref=dst, send_sem=send, recv_sem=recv,
            device_id=where, device_id_type=MESH,
        )

    def cols(side, ch):
        return pl.ds(pl.multiple_of(side * half + ch * width, width), width)

    barrier = pltpu.get_barrier_semaphore()
    for d in range(1, total):
        pl.semaphore_signal(
            barrier, inc=1, device_id={"hist": (me + d) % total}, device_id_type=MESH
        )
    pl.semaphore_signal(barrier, inc=1, device_id={"chan": 1 - core}, device_id_type=MESH)
    pl.semaphore_signal(barrier, inc=1, device_id={"seq": 1 - seq}, device_id_type=MESH)

    own = []
    for ch in range(chunks):
        own.append((
            pltpu.make_async_copy(taps_ref.at[:, cols(q, ch)], taps_buf.at[q, ch], own_sem.at[0, ch]),
            pltpu.make_async_copy(hist_ref.at[:, cols(q, ch)], hist_buf.at[q, ch], own_sem.at[1, ch]),
        ))
        for copy in own[-1]:
            copy.start()
    gate_side = pl.ds(pl.multiple_of(q * half, half), half)
    gate_other = pl.ds(pl.multiple_of((1 - q) * half, half), half)
    loads = [
        pltpu.make_async_copy(fwd_ref, fwd_buf, load_sem.at[0]),
        pltpu.make_async_copy(inv_ref, inv_buf, load_sem.at[1]),
        pltpu.make_async_copy(gate_ref.at[:, gate_side], gate_buf.at[q], load_sem.at[2]),
        pltpu.make_async_copy(weight_ref, weight_buf, load_sem.at[3]),
    ]
    for copy in loads:
        copy.start()

    @pl.when(p == pairs - 1)
    def _():
        taps_buf[2] = jnp.zeros(taps_buf.shape[1:], BF16)

    pl.semaphore_wait(barrier, total + 1)

    xt, xh, zt, xf, xz = [], [], [], [], []
    for j in range(chunks // 2):
        mine = 2 * j + seq
        xt.append(remote(taps_ref.at[:, cols(1 - q, mine)], taps_buf.at[q, mine],
                         xt_send.at[j], xt_recv.at[j], {"hist": partner}))
        xt[-1].start()
        before = {"hist": jnp.maximum(me - 2, 0)}
        zt.append(remote(taps_buf.at[0, mine], taps_buf.at[2, mine],
                         zt_send.at[j], zt_recv.at[j], before))
        xf.append(remote(taps_buf.at[1 - q, mine], taps_buf.at[1 - q, mine],
                         xf_send.at[j], xf_recv.at[j], {"seq": 1 - seq}))
        xz.append(remote(taps_buf.at[2, mine], taps_buf.at[2, mine],
                         xz_send.at[j], xz_recv.at[j], {"seq": 1 - seq}))

        @pl.when((q == 0) & (p > 0))
        def _():
            remote(taps_ref.at[:, cols(0, mine)], taps_buf.at[2, mine],
                   zt_send.at[j], zt_recv.at[j], before).start()

    for ch in range(chunks):
        xh.append(remote(hist_ref.at[:, cols(1 - q, ch)], hist_buf.at[q, ch],
                         xh_send.at[ch], xh_recv.at[ch], {"hist": partner}))
        xh[-1].start()
        if ch == 0:
            xg = remote(gate_ref.at[:, gate_other], gate_buf.at[q], xg_send, xg_recv,
                        {"hist": partner})
            xg.start()
    for j in range(chunks // 2):
        xt[j].wait_recv()
        xf[j].start()

        @pl.when((q == 1) & (p > 0))
        def _():
            zt[j].start()

    for j in range(chunks // 2):
        @pl.when(p < pairs - 1)
        def _():
            zt[j].wait_recv()
            xz[j].start()

    loads[0].wait()
    loads[1].wait()

    rs, az, ay = {}, {}, {}

    def compute(ch):
        for copy in own[ch]:
            copy.wait()
        if ch % 2 == 0:
            xf[ch // 2].wait_recv()

            @pl.when(p < pairs - 1)
            def _():
                xz[ch // 2].wait_recv()

        t0, t1, t2 = (taps_buf[i, ch] for i in range(3))
        first = fwd_buf[:, :rows]
        second = fwd_buf[:, rows:]
        s_a = dot(first, t0) + dot(second, t1)
        s_b = dot(first, t1) + dot(second, t2)
        xh[ch].wait_recv()
        h_a = dot(first, hist_buf[0, ch])
        h_b = dot(first, hist_buf[1, ch])
        ra, ia = spectrum_product(s_a, h_a)
        rb, ib = spectrum_product(s_b, h_b)
        conv = dot(inv_buf[:, :modes], (ra + rb).astype(BF16)) + dot(
            inv_buf[:, modes:], (ia + ib).astype(BF16)
        )
        conv = conv.reshape(pairs, conv.shape[0] // pairs, width)
        send_buf[ch] = conv.astype(BF16)
        own_buf[ch] = conv
        for d in range(1, pairs):
            to = (p + d) % pairs
            rs[ch, d] = remote(send_buf.at[ch, to], recv_buf.at[ch, d - 1],
                               rs_send.at[ch, d - 1], rs_recv.at[ch, d - 1],
                               {"hist": 2 * to + q})
            rs[ch, d].start()

    def reduce(ch):
        if ch == 0:
            loads[2].wait()
            xg.wait_recv()
        value = own_buf[ch, p]
        for d in range(1, pairs):
            rs[ch, d].wait_recv()
            value = value + recv_buf[ch, d - 1].astype(F32)
        gates = gate_buf[:, :, ch * width:(ch + 1) * width].astype(F32)
        gated = (value * gates.reshape(value.shape)).astype(BF16)
        gated_buf[ch, q, p] = gated
        slot = gated_buf.at[ch, q, p]
        for d in range(1, pairs):
            az[ch, d] = remote(slot, slot, az_send.at[ch, d - 1], az_recv.at[ch, d - 1],
                               {"hist": 2 * ((p + d) % pairs) + q})
            az[ch, d].start()
        ay[ch, 0] = remote(slot, slot, ay_send.at[ch, 0], ay_recv.at[ch, 0], {"hist": partner})
        ay[ch, 0].start()

    def forward(ch):
        for d in range(1, pairs):
            az[ch, d].wait_recv()
            slot = gated_buf.at[ch, q, (p - d + pairs) % pairs]
            ay[ch, d] = remote(slot, slot, ay_send.at[ch, d], ay_recv.at[ch, d], {"hist": partner})
            ay[ch, d].start()

    def project(ch):
        if ch == 0:
            loads[3].wait()
        for d in range(pairs):
            ay[ch, d].wait_recv()
        low = gated_buf[ch, 0].reshape(-1, width)
        high = gated_buf[ch, 1].reshape(-1, width)
        value = dot(low, weight_buf[ch * width:(ch + 1) * width]) + dot(
            high, weight_buf[half + ch * width:half + (ch + 1) * width]
        )
        value = value.reshape(acc_buf.shape)
        if ch == 0:
            acc_buf[...] = value
        else:
            acc_buf[...] += value

    for step in range(chunks + 3):
        if step < chunks:
            compute(step)
        if 0 <= step - 1 < chunks:
            reduce(step - 1)
        if 0 <= step - 2 < chunks:
            forward(step - 2)
        if 0 <= step - 3 < chunks:
            project(step - 3)

    swap_send[...] = acc_buf[:, 1 - core].astype(BF16)
    swap = remote(swap_send, swap_recv, sw_send, sw_recv, {"chan": 1 - core})
    swap.start()
    swap.wait_recv()
    fin_buf[...] = (acc_buf[:, core] + swap_recv[...].astype(F32)).astype(BF16)
    fin = []
    for d in range(1, total):
        to = (me + d) % total
        fin.append(remote(fin_buf.at[to], res_buf.at[me], fin_send.at[d - 1], fin_recv.at[d - 1],
                          {"hist": to}))
        fin[-1].start()
    res_buf[me] = fin_buf[me]

    for ch in range(chunks):
        xh[ch].wait_send()
    for j in range(chunks // 2):
        xt[j].wait_send()
        xf[j].wait_send()

        @pl.when(p > 0)
        def _():
            zt[j].wait_send()

        @pl.when(p < pairs - 1)
        def _():
            xz[j].wait_send()

    xg.wait_send()
    for group in (rs, az, ay):
        for copy in group.values():
            copy.wait_send()
    swap.wait_send()
    for copy in fin:
        copy.wait_recv()
    for k in range(total):
        out_ref[:, k * columns:(k + 1) * columns] = res_buf[k]
    for copy in fin:
        copy.wait_send()


def local_kernel(chunks, history, filter_taps, gate_values, out_weight):
    rows, channels = history.shape
    owned = gate_values.shape[0]
    total = lax.axis_size("hist")
    cores = lax.axis_size("chan")
    pairs = total // 2
    tokens = owned * total
    half = channels // 2
    width = half // chunks
    columns = out_weight.shape[1]
    part = owned // cores
    forward, inverse = tables(rows, tokens)
    modes2 = forward.shape[0]
    forward = jnp.asarray(forward, F32).astype(BF16)
    inverse = jnp.asarray(inverse, F32).astype(BF16)
    dma = pltpu.SemaphoreType.DMA
    others = pairs - 1
    scratch = [
        pltpu.VMEM((3, chunks, rows, width), BF16),
        pltpu.VMEM((2, chunks, rows, width), BF16),
        pltpu.VMEM((2, owned, half), BF16),
        pltpu.VMEM(out_weight.shape, BF16),
        pltpu.VMEM(forward.shape, BF16),
        pltpu.VMEM(inverse.shape, BF16),
        pltpu.VMEM((chunks, pairs, 2 * owned, width), BF16),
        pltpu.VMEM((chunks, pairs, 2 * owned, width), F32),
        pltpu.VMEM((chunks, others, 2 * owned, width), BF16),
        pltpu.VMEM((chunks, 2, pairs, 2 * owned, width), BF16),
        pltpu.VMEM((total, cores, part, columns), F32),
        pltpu.VMEM((total, part, columns), BF16),
        pltpu.VMEM((total, part, columns), BF16),
        pltpu.VMEM((total, part, columns), BF16),
        pltpu.VMEM((total, part, columns), BF16),
        dma((4,)), dma((2, chunks)),
        dma((chunks // 2,)), dma((chunks // 2,)), dma((chunks,)), dma((chunks,)), dma, dma,
        dma((chunks // 2,)), dma((chunks // 2,)), dma((chunks // 2,)), dma((chunks // 2,)),
        dma((chunks // 2,)), dma((chunks // 2,)),
        dma((chunks, others)), dma((chunks, others)),
        dma((chunks, others)), dma((chunks, others)),
        dma((chunks, pairs)), dma((chunks, pairs)),
        dma, dma, dma((total - 1,)), dma((total - 1,)),
    ]
    return pl.pallas_call(
        functools.partial(kernel, pairs, chunks),
        out_shape=jax.ShapeDtypeStruct((part, total * columns), BF16),
        in_specs=[pl.BlockSpec(memory_space=pl.ANY)] * 6,
        out_specs=pl.BlockSpec(memory_space=pltpu.VMEM),
        scratch_shapes=scratch,
        compiler_params=pltpu.CompilerParams(
            collective_id=0, has_side_effects=True, vmem_limit_bytes=67043328
        ),
    )(history, filter_taps, gate_values, out_weight, forward, inverse)


def local(history, filter_taps, gate_values, out_weight):
    rows, channels = history.shape
    owned = gate_values.shape[0]
    total = lax.axis_size("hist")
    cores = lax.axis_size("chan")
    fits = (
        total % 2 == 0
        and total >= 4
        and cores == 2
        and lax.axis_size("seq") == 2
        and CHUNKS % 2 == 0
        and owned % (16 * cores) == 0
        and rows == owned * total
        and channels % (256 * CHUNKS) == 0
        and out_weight.shape[1] % 128 == 0
    )
    if fits:
        return local_kernel(CHUNKS, history, filter_taps, gate_values, out_weight)
    return local_general(history, filter_taps, gate_values, out_weight)


def solution(mesh):
    return jax.shard_map(
        local,
        mesh=mesh,
        in_specs=(
            P(("seq", "hist"), "chan"),
            P("hist", "chan"),
            P(("seq", "hist"), "chan"),
            P("chan", "hist"),
        ),
        out_specs=P(("seq", "hist", "chan"), None),
        check_vma=False,
    )
```

```python
import functools
import math

import jax
import jax.numpy as jnp
import numpy as np
from jax import lax
from jax.experimental import pallas as pl
from jax.experimental.pallas import tpu as pltpu
from jax.sharding import PartitionSpec as P

MESH = pl.DeviceIdType.MESH
BF16 = jnp.bfloat16
F32 = jnp.float32
CHUNKS = 4
WINDOW = 3
REDUCE_AT = 1.1
LINE_STEP = 1.01


def tables(local_rows, block_tokens):
    period = local_rows + block_tokens
    modes = period // 2
    odd = 2 * np.arange(modes) + 1
    turn = math.pi / period
    places = np.arange(period)
    phase = (np.outer(odd, places) % (2 * period)) * turn
    forward = np.concatenate([np.cos(phase), np.sin(phase)], 0)
    lags = block_tokens - 1 - np.arange(block_tokens)
    phase = (np.outer(lags, odd) % (2 * period)) * turn
    inverse = np.concatenate([np.cos(phase), -np.sin(phase)], 1) * (2.0 / period)
    return forward, inverse


def spectrum_product(taps, values):
    half = taps.shape[0] // 2
    tc, ts, vc, vs = taps[:half], taps[half:], values[:half], values[half:]
    return tc * vc + ts * vs, tc * vs - ts * vc


def dot(a, b):
    return jnp.dot(a, b, preferred_element_type=F32)


def local_general(history, filter_taps, gate_values, out_weight):
    local_rows, channels = history.shape
    owned_rows = gate_values.shape[0]
    count_hist = lax.axis_size("hist")
    count_chan = lax.axis_size("chan")
    block_tokens = owned_rows * count_hist
    forward, inverse = tables(local_rows, block_tokens)
    forward = jnp.asarray(forward, F32)
    forward_high = forward.astype(BF16)
    forward_low = (forward - forward_high.astype(F32)).astype(BF16)
    inverse = jnp.asarray(inverse, F32)
    next_taps = lax.ppermute(
        filter_taps, "hist", [(source, source - 1) for source in range(1, count_hist)]
    )
    extended = jnp.concatenate([filter_taps, next_taps], 0)[: forward.shape[1]]
    spec_taps = dot(forward_high, extended) + dot(forward_low, extended)
    spec_input = dot(forward_high[:, :local_rows], history) + dot(
        forward_low[:, :local_rows], history
    )
    spectrum = jnp.concatenate(spectrum_product(spec_taps, spec_input), 0)
    partial_conv = jnp.dot(
        inverse, spectrum, precision=lax.Precision.HIGHEST, preferred_element_type=F32
    )
    conv = lax.psum_scatter(partial_conv, "hist", scatter_dimension=0, tiled=True)
    gated = (conv * gate_values.astype(F32)).astype(BF16)
    partial_value = dot(lax.all_gather(gated, "hist", axis=0, tiled=True), out_weight)
    columns = partial_value.shape[1]
    half_rows = owned_rows // count_chan
    ordered = partial_value.reshape(count_hist, count_chan, half_rows, columns)
    ordered = ordered.transpose(1, 0, 2, 3).reshape(-1, columns)
    summed = lax.psum_scatter(ordered.astype(BF16), "chan", scatter_dimension=0, tiled=True)
    return lax.all_to_all(summed, "hist", split_axis=0, concat_axis=1, tiled=True)


def kernel(
    pairs, chunks, hist_ref, taps_ref, gate_ref, weight_ref, fwd_ref, inv_ref, out_ref,
    taps_buf, hist_buf, gate_buf, weight_buf, fwd_buf, inv_buf,
    send_buf, own_buf, recv_buf, gated_buf, acc_buf, swap_send, swap_recv, fin_buf, res_buf,
    load_sem, own_sem, xt_send, xt_recv, xh_send, xh_recv, xg_send, xg_recv,
    zt_send, zt_recv, xf_send, xf_recv, rs_send, rs_recv, az_send, az_recv, ay_send, ay_recv,
    sw_send, sw_recv, fin_send, fin_recv, ready_sem,
):
    me = lax.axis_index("hist")
    core = lax.axis_index("chan")
    seq = lax.axis_index("seq")
    p = me // 2
    q = me % 2
    total = 2 * pairs
    rows = hist_ref.shape[0]
    half = hist_ref.shape[1] // 2
    width = half // chunks
    columns = weight_ref.shape[1]
    partner = 2 * p + (1 - q)
    modes = fwd_buf.shape[0] // 2

    def remote(src, dst, send, recv, where):
        return pltpu.make_async_remote_copy(
            src_ref=src, dst_ref=dst, send_sem=send, recv_sem=recv,
            device_id=where, device_id_type=MESH,
        )

    def cols(side, ch):
        return pl.ds(pl.multiple_of(side * half + ch * width, width), width)

    barrier = pltpu.get_barrier_semaphore()
    def greet_line(sem):
        @pl.when(p > 0)
        def _():
            pl.semaphore_signal(sem, inc=1, device_id={"hist": me - 2}, device_id_type=MESH)

        @pl.when(p < pairs - 1)
        def _():
            pl.semaphore_signal(sem, inc=1, device_id={"hist": me + 2}, device_id_type=MESH)

    beside = jnp.minimum(p, 1) + jnp.minimum(pairs - 1 - p, 1)
    greet_line(barrier)
    pl.semaphore_signal(barrier, inc=1, device_id={"hist": partner}, device_id_type=MESH)
    pl.semaphore_signal(barrier, inc=1, device_id={"chan": 1 - core}, device_id_type=MESH)
    pl.semaphore_signal(barrier, inc=1, device_id={"seq": 1 - seq}, device_id_type=MESH)

    own = []
    for ch in range(chunks):
        own.append((
            pltpu.make_async_copy(taps_ref.at[:, cols(q, ch)], taps_buf.at[q, ch], own_sem.at[0, ch]),
            pltpu.make_async_copy(hist_ref.at[:, cols(q, ch)], hist_buf.at[q, ch], own_sem.at[1, ch]),
        ))
        for copy in own[-1]:
            copy.start()
    gate_side = pl.ds(pl.multiple_of(q * half, half), half)
    gate_other = pl.ds(pl.multiple_of((1 - q) * half, half), half)
    loads = [
        pltpu.make_async_copy(fwd_ref, fwd_buf, load_sem.at[0]),
        pltpu.make_async_copy(inv_ref, inv_buf, load_sem.at[1]),
        pltpu.make_async_copy(gate_ref.at[:, gate_side], gate_buf.at[q], load_sem.at[2]),
        pltpu.make_async_copy(weight_ref, weight_buf, load_sem.at[3]),
    ]
    for copy in loads:
        copy.start()

    @pl.when((q == 0) & (p == pairs - 1))
    def _():
        taps_buf[2] = jnp.zeros(taps_buf.shape[1:], BF16)

    @pl.when((q == 1) & (p == 0))
    def _():
        hist_buf[2] = jnp.zeros(hist_buf.shape[1:], BF16)

    pl.semaphore_wait(barrier, 3 + beside)

    xt, xh, zt, xf = [], [], [], []
    for j in range(chunks // 2):
        mine = 2 * j + seq
        xt.append(remote(taps_ref.at[:, cols(1 - q, mine)], taps_buf.at[q, mine],
                         xt_send.at[j], xt_recv.at[j], {"hist": partner}))
        xf.append(remote(taps_buf.at[1 - q, mine], taps_buf.at[1 - q, mine],
                         xf_send.at[j], xf_recv.at[j], {"seq": 1 - seq}))

    for ch in range(chunks):
        low = remote(taps_ref.at[:, cols(0, ch)], taps_buf.at[2, ch], zt_send.at[ch],
                     zt_recv.at[ch], {"hist": jnp.maximum(me - 2, 0)})
        high = remote(hist_ref.at[:, cols(1, ch)], hist_buf.at[2, ch], zt_send.at[ch],
                      zt_recv.at[ch], {"hist": jnp.minimum(me + 2, total - 1)})
        zt.append((low, high))

        @pl.when((q == 0) & (p > 0))
        def _():
            low.start()

        @pl.when((q == 1) & (p < pairs - 1))
        def _():
            high.start()

    for ch in range(chunks):
        xh.append(remote(hist_ref.at[:, cols(1 - q, ch)], hist_buf.at[q, ch],
                         xh_send.at[ch], xh_recv.at[ch], {"hist": partner}))
    xg = remote(gate_ref.at[:, gate_other], gate_buf.at[q], xg_send, xg_recv, {"hist": partner})
    queue = [(copy,) for copy in xt] + [(copy,) for copy in xh]
    queue[len(xt) + 1] += (xg,)

    def advance(i):
        if i < len(queue):
            for copy in queue[i]:
                copy.start()

    for i in range(WINDOW):
        advance(i)
    for r in range(pairs - 2):
        greet_line(ready_sem.at[r])
        pl.semaphore_wait(ready_sem.at[r], beside)

    for j in range(chunks // 2):
        xt[j].wait_recv()
        advance(j + WINDOW)
        xf[j].start()

    loads[0].wait()
    loads[1].wait()

    rs, up, down, ay = {}, {}, {}, {}

    def compute(ch):
        for copy in own[ch]:
            copy.wait()
        if ch % 2 == 0:
            xf[ch // 2].wait_recv()


        @pl.when((q == 0) & (p < pairs - 1))
        def _():
            zt[ch][0].wait_recv()

        @pl.when((q == 1) & (p > 0))
        def _():
            zt[ch][1].wait_recv()

        t0, t1 = taps_buf[0, ch], taps_buf[1, ch]
        first = fwd_buf[:, :rows]
        second = fwd_buf[:, rows:]
        s_a = dot(first, t0) + dot(second, t1)
        s_b = dot(first, t1)
        s_c = dot(second, taps_buf[2 - 2 * q, ch])
        xh[ch].wait_recv()
        advance(len(xt) + ch + WINDOW)
        h_a = dot(first, hist_buf[0, ch])
        h_b = dot(first, hist_buf[1, ch])
        h_c = dot(first, hist_buf[1 + q, ch])
        ra, ia = spectrum_product(s_a, h_a)
        rb, ib = spectrum_product(s_b, h_b)
        rc, ic = spectrum_product(s_c, h_c)
        conv = dot(inv_buf[:, :modes], (ra + rb + rc).astype(BF16)) + dot(
            inv_buf[:, modes:], (ia + ib + ic).astype(BF16)
        )
        conv = conv.reshape(pairs, conv.shape[0] // pairs, width)
        send_buf[ch] = conv.astype(BF16)
        own_buf[ch] = conv
        for d in range(1, pairs):
            to = (p + d) % pairs
            rs[ch, d] = remote(send_buf.at[ch, to], recv_buf.at[ch, d - 1],
                               rs_send.at[ch, d - 1], rs_recv.at[ch, d - 1],
                               {"hist": 2 * to + q})
            rs[ch, d].start()

    def reduce(ch):
        if ch == 0:
            loads[2].wait()
            xg.wait_recv()
        value = own_buf[ch, p]
        for d in range(1, pairs):
            rs[ch, d].wait_recv()
            value = value + recv_buf[ch, d - 1].astype(F32)
        gates = gate_buf[:, :, ch * width:(ch + 1) * width].astype(F32)
        gated = (value * gates.reshape(value.shape)).astype(BF16)
        gated_buf[ch, q, p] = gated
        line(ch, 0)

    def line(ch, s):
        if s > 0:
            left_slot = gated_buf.at[ch, q, (p - s + pairs) % pairs]
            right_slot = gated_buf.at[ch, q, (p + s) % pairs]
        else:
            left_slot = right_slot = gated_buf.at[ch, q, p]
        below = {"hist": jnp.maximum(me - 2, 0)}
        above = {"hist": jnp.minimum(me + 2, total - 1)}
        across = {"hist": partner}
        up[ch, s] = remote(left_slot, left_slot, az_send.at[ch, 0, s], az_recv.at[ch, 0, s], above)
        down[ch, s] = remote(right_slot, right_slot, az_send.at[ch, 1, s], az_recv.at[ch, 1, s], below)
        ay[ch, 0, s] = remote(left_slot, left_slot, ay_send.at[ch, 0, s], ay_recv.at[ch, 0, s], across)
        ay[ch, 1, s] = remote(right_slot, right_slot, ay_send.at[ch, 1, s], ay_recv.at[ch, 1, s], across)

        @pl.when(p - s >= 0)
        def _():
            if s > 0:
                up[ch, s - 1].wait_recv()

            @pl.when(p < pairs - 1)
            def _():
                up[ch, s].start()

            ay[ch, 0, s].start()

        @pl.when(p + s < pairs)
        def _():
            if s > 0:
                down[ch, s - 1].wait_recv()

            @pl.when(p > 0)
            def _():
                down[ch, s].start()

            if s > 0:
                ay[ch, 1, s].start()

    def project(ch):
        if ch == 0:
            loads[3].wait()
        ay[ch, 0, 0].wait_recv()
        for s in range(1, pairs):
            @pl.when(p - s >= 0)
            def _():
                ay[ch, 0, s].wait_recv()

            @pl.when(p + s < pairs)
            def _():
                ay[ch, 1, s].wait_recv()

        low = gated_buf[ch, 0].reshape(-1, width)
        high = gated_buf[ch, 1].reshape(-1, width)
        value = dot(low, weight_buf[ch * width:(ch + 1) * width]) + dot(
            high, weight_buf[half + ch * width:half + (ch + 1) * width]
        )
        value = value.reshape(acc_buf.shape)
        if ch == 0:
            acc_buf[...] = value
        else:
            acc_buf[...] += value

    events = []
    for ch in range(chunks):
        events.append((ch, 0, functools.partial(compute, ch)))
        events.append((ch + REDUCE_AT, 1, functools.partial(reduce, ch)))
        for s in range(1, pairs):
            events.append((ch + REDUCE_AT + s * LINE_STEP, 1 + s, functools.partial(line, ch, s)))
        events.append((ch + REDUCE_AT + pairs * LINE_STEP, 1 + pairs, functools.partial(project, ch)))
    for event in sorted(events, key=lambda entry: entry[:2]):
        event[2]()

    swap_send[...] = acc_buf[:, 1 - core].astype(BF16)
    swap = remote(swap_send, swap_recv, sw_send, sw_recv, {"chan": 1 - core})
    swap.start()
    swap.wait_recv()
    fin_buf[...] = (acc_buf[:, core] + swap_recv[...].astype(F32)).astype(BF16)
    fin = []
    for d in range(1, total):
        to = (me + d) % total
        fin.append(remote(fin_buf.at[to], res_buf.at[me], fin_send.at[d - 1], fin_recv.at[d - 1],
                          {"hist": to}))
        fin[-1].start()
    res_buf[me] = fin_buf[me]

    for ch in range(chunks):
        xh[ch].wait_send()
    for j in range(chunks // 2):
        xt[j].wait_send()
        xf[j].wait_send()
    for ch in range(chunks):
        @pl.when((q == 0) & (p > 0))
        def _():
            zt[ch][0].wait_send()

        @pl.when((q == 1) & (p < pairs - 1))
        def _():
            zt[ch][1].wait_send()

    xg.wait_send()
    for copy in rs.values():
        copy.wait_send()
    for ch in range(chunks):
        ay[ch, 0, 0].wait_send()
        for s in range(pairs):
            @pl.when(p - s >= 0)
            def _():
                if s > 0:
                    ay[ch, 0, s].wait_send()

                @pl.when(p < pairs - 1)
                def _():
                    up[ch, s].wait_send()

            @pl.when(p + s < pairs)
            def _():
                if s > 0:
                    ay[ch, 1, s].wait_send()

                @pl.when(p > 0)
                def _():
                    down[ch, s].wait_send()

    swap.wait_send()
    for copy in fin:
        copy.wait_recv()
    for k in range(total):
        out_ref[:, k * columns:(k + 1) * columns] = res_buf[k]
    for copy in fin:
        copy.wait_send()


def local_kernel(chunks, history, filter_taps, gate_values, out_weight):
    rows, channels = history.shape
    owned = gate_values.shape[0]
    total = lax.axis_size("hist")
    cores = lax.axis_size("chan")
    pairs = total // 2
    tokens = owned * total
    half = channels // 2
    width = half // chunks
    columns = out_weight.shape[1]
    part = owned // cores
    forward, inverse = tables(rows, tokens)
    modes2 = forward.shape[0]
    forward = jnp.asarray(forward, F32).astype(BF16)
    inverse = jnp.asarray(inverse, F32).astype(BF16)
    dma = pltpu.SemaphoreType.DMA
    others = pairs - 1
    scratch = [
        pltpu.VMEM((3, chunks, rows, width), BF16),
        pltpu.VMEM((3, chunks, rows, width), BF16),
        pltpu.VMEM((2, owned, half), BF16),
        pltpu.VMEM(out_weight.shape, BF16),
        pltpu.VMEM(forward.shape, BF16),
        pltpu.VMEM(inverse.shape, BF16),
        pltpu.VMEM((chunks, pairs, 2 * owned, width), BF16),
        pltpu.VMEM((chunks, pairs, 2 * owned, width), F32),
        pltpu.VMEM((chunks, others, 2 * owned, width), BF16),
        pltpu.VMEM((chunks, 2, pairs, 2 * owned, width), BF16),
        pltpu.VMEM((total, cores, part, columns), F32),
        pltpu.VMEM((total, part, columns), BF16),
        pltpu.VMEM((total, part, columns), BF16),
        pltpu.VMEM((total, part, columns), BF16),
        pltpu.VMEM((total, part, columns), BF16),
        dma((4,)), dma((2, chunks)),
        dma((chunks // 2,)), dma((chunks // 2,)), dma((chunks,)), dma((chunks,)), dma, dma,
        dma((chunks,)), dma((chunks,)), dma((chunks // 2,)), dma((chunks // 2,)),
        dma((chunks, others)), dma((chunks, others)),
        dma((chunks, 2, pairs)), dma((chunks, 2, pairs)),
        dma((chunks, 2, pairs)), dma((chunks, 2, pairs)),
        dma, dma, dma((total - 1,)), dma((total - 1,)),
        pltpu.SemaphoreType.REGULAR((pairs - 2,)),
    ]
    return pl.pallas_call(
        functools.partial(kernel, pairs, chunks),
        out_shape=jax.ShapeDtypeStruct((part, total * columns), BF16),
        in_specs=[pl.BlockSpec(memory_space=pl.ANY)] * 6,
        out_specs=pl.BlockSpec(memory_space=pltpu.VMEM),
        scratch_shapes=scratch,
        compiler_params=pltpu.CompilerParams(
            collective_id=0, has_side_effects=True, vmem_limit_bytes=67043328
        ),
    )(history, filter_taps, gate_values, out_weight, forward, inverse)


def local(history, filter_taps, gate_values, out_weight):
    rows, channels = history.shape
    owned = gate_values.shape[0]
    total = lax.axis_size("hist")
    cores = lax.axis_size("chan")
    fits = (
        total % 2 == 0
        and total >= 6
        and cores == 2
        and lax.axis_size("seq") == 2
        and CHUNKS % 2 == 0
        and owned % (16 * cores) == 0
        and rows == owned * total
        and channels % (128 * CHUNKS) == 0
        and out_weight.shape[1] % 128 == 0
    )
    if fits:
        return local_kernel(CHUNKS, history, filter_taps, gate_values, out_weight)
    return local_general(history, filter_taps, gate_values, out_weight)


def solution(mesh):
    return jax.shard_map(
        local,
        mesh=mesh,
        in_specs=(
            P(("seq", "hist"), "chan"),
            P("hist", "chan"),
            P(("seq", "hist"), "chan"),
            P("chan", "hist"),
        ),
        out_specs=P(("seq", "hist", "chan"), None),
        check_vma=False,
    )
```

```python
import functools
import math

import jax
import jax.numpy as jnp
import numpy as np
from jax import lax
from jax.experimental import pallas as pl
from jax.experimental.pallas import tpu as pltpu
from jax.sharding import PartitionSpec as P

MESH = pl.DeviceIdType.MESH
BF16 = jnp.bfloat16
F32 = jnp.float32
CHUNKS = 4
WINDOW = 3
REDUCE_AT = 1.1
LINE_STEP = 1.95


def tables(local_rows, block_tokens):
    period = local_rows + block_tokens
    modes = period // 2
    odd = 2 * np.arange(modes) + 1
    turn = math.pi / period
    places = np.arange(period)
    phase = (np.outer(odd, places) % (2 * period)) * turn
    forward = np.concatenate([np.cos(phase), np.sin(phase)], 0)
    lags = block_tokens - 1 - np.arange(block_tokens)
    phase = (np.outer(lags, odd) % (2 * period)) * turn
    inverse = np.concatenate([np.cos(phase), -np.sin(phase)], 1) * (2.0 / period)
    return forward, inverse


def spectrum_product(taps, values):
    half = taps.shape[0] // 2
    tc, ts, vc, vs = taps[:half], taps[half:], values[:half], values[half:]
    return tc * vc + ts * vs, tc * vs - ts * vc


def dot(a, b):
    return jnp.dot(a, b, preferred_element_type=F32)


def local_general(history, filter_taps, gate_values, out_weight):
    local_rows, channels = history.shape
    owned_rows = gate_values.shape[0]
    count_hist = lax.axis_size("hist")
    count_chan = lax.axis_size("chan")
    block_tokens = owned_rows * count_hist
    forward, inverse = tables(local_rows, block_tokens)
    forward = jnp.asarray(forward, F32)
    forward_high = forward.astype(BF16)
    forward_low = (forward - forward_high.astype(F32)).astype(BF16)
    inverse = jnp.asarray(inverse, F32)
    next_taps = lax.ppermute(
        filter_taps, "hist", [(source, source - 1) for source in range(1, count_hist)]
    )
    extended = jnp.concatenate([filter_taps, next_taps], 0)[: forward.shape[1]]
    spec_taps = dot(forward_high, extended) + dot(forward_low, extended)
    spec_input = dot(forward_high[:, :local_rows], history) + dot(
        forward_low[:, :local_rows], history
    )
    spectrum = jnp.concatenate(spectrum_product(spec_taps, spec_input), 0)
    partial_conv = jnp.dot(
        inverse, spectrum, precision=lax.Precision.HIGHEST, preferred_element_type=F32
    )
    conv = lax.psum_scatter(partial_conv, "hist", scatter_dimension=0, tiled=True)
    gated = (conv * gate_values.astype(F32)).astype(BF16)
    partial_value = dot(lax.all_gather(gated, "hist", axis=0, tiled=True), out_weight)
    columns = partial_value.shape[1]
    half_rows = owned_rows // count_chan
    ordered = partial_value.reshape(count_hist, count_chan, half_rows, columns)
    ordered = ordered.transpose(1, 0, 2, 3).reshape(-1, columns)
    summed = lax.psum_scatter(ordered.astype(BF16), "chan", scatter_dimension=0, tiled=True)
    return lax.all_to_all(summed, "hist", split_axis=0, concat_axis=1, tiled=True)


def kernel(
    pairs, chunks, hist_ref, taps_ref, gate_ref, weight_ref, fwd_ref, inv_ref, out_ref,
    taps_buf, hist_buf, gate_buf, weight_buf, fwd_buf, inv_buf,
    send_buf, own_buf, recv_buf, gated_buf, acc_buf, swap_send, swap_recv, fin_buf, res_buf,
    load_sem, own_sem, xt_send, xt_recv, xh_send, xh_recv, xg_send, xg_recv,
    zt_send, zt_recv, xf_send, xf_recv, rs_send, rs_recv, az_send, az_recv, ay_send, ay_recv,
    sw_send, sw_recv, fin_send, fin_recv, ready_sem,
):
    me = lax.axis_index("hist")
    core = lax.axis_index("chan")
    seq = lax.axis_index("seq")
    p = me // 2
    q = me % 2
    total = 2 * pairs
    rows = hist_ref.shape[0]
    half = hist_ref.shape[1] // 2
    width = half // chunks
    columns = weight_ref.shape[1]
    partner = 2 * p + (1 - q)
    modes = fwd_buf.shape[0] // 2

    def remote(src, dst, send, recv, where):
        return pltpu.make_async_remote_copy(
            src_ref=src, dst_ref=dst, send_sem=send, recv_sem=recv,
            device_id=where, device_id_type=MESH,
        )

    def cols(side, ch):
        return pl.ds(pl.multiple_of(side * half + ch * width, width), width)

    barrier = pltpu.get_barrier_semaphore()
    def greet_line(sem):
        @pl.when(p > 0)
        def _():
            pl.semaphore_signal(sem, inc=1, device_id={"hist": me - 2}, device_id_type=MESH)

        @pl.when(p < pairs - 1)
        def _():
            pl.semaphore_signal(sem, inc=1, device_id={"hist": me + 2}, device_id_type=MESH)

    beside = jnp.minimum(p, 1) + jnp.minimum(pairs - 1 - p, 1)
    greet_line(barrier)
    pl.semaphore_signal(barrier, inc=1, device_id={"hist": partner}, device_id_type=MESH)
    pl.semaphore_signal(barrier, inc=1, device_id={"chan": 1 - core}, device_id_type=MESH)
    pl.semaphore_signal(barrier, inc=1, device_id={"seq": 1 - seq}, device_id_type=MESH)

    own = []
    for ch in range(chunks):
        own.append((
            pltpu.make_async_copy(taps_ref.at[:, cols(q, ch)], taps_buf.at[q, ch], own_sem.at[0, ch]),
            pltpu.make_async_copy(hist_ref.at[:, cols(q, ch)], hist_buf.at[q, ch], own_sem.at[1, ch]),
        ))
        for copy in own[-1]:
            copy.start()
    gate_side = pl.ds(pl.multiple_of(q * half, half), half)
    gate_other = pl.ds(pl.multiple_of((1 - q) * half, half), half)
    loads = [
        pltpu.make_async_copy(fwd_ref, fwd_buf, load_sem.at[0]),
        pltpu.make_async_copy(inv_ref, inv_buf, load_sem.at[1]),
        pltpu.make_async_copy(gate_ref.at[:, gate_side], gate_buf.at[q], load_sem.at[2]),
        pltpu.make_async_copy(weight_ref, weight_buf, load_sem.at[3]),
    ]
    for copy in loads:
        copy.start()

    @pl.when((q == 0) & (p == pairs - 1))
    def _():
        taps_buf[2] = jnp.zeros(taps_buf.shape[1:], BF16)

    @pl.when((q == 1) & (p == 0))
    def _():
        hist_buf[2] = jnp.zeros(hist_buf.shape[1:], BF16)

    pl.semaphore_wait(barrier, 3 + beside)

    xt, xh, zt, xf = [], [], [], []
    for j in range(chunks // 2):
        mine = 2 * j + seq
        xt.append(remote(taps_ref.at[:, cols(1 - q, mine)], taps_buf.at[q, mine],
                         xt_send.at[j], xt_recv.at[j], {"hist": partner}))
        xf.append(remote(taps_buf.at[1 - q, mine], taps_buf.at[1 - q, mine],
                         xf_send.at[j], xf_recv.at[j], {"seq": 1 - seq}))

    for ch in range(chunks):
        low = remote(taps_ref.at[:, cols(0, ch)], taps_buf.at[2, ch], zt_send.at[ch],
                     zt_recv.at[ch], {"hist": jnp.maximum(me - 2, 0)})
        high = remote(hist_ref.at[:, cols(1, ch)], hist_buf.at[2, ch], zt_send.at[ch],
                      zt_recv.at[ch], {"hist": jnp.minimum(me + 2, total - 1)})
        zt.append((low, high))

        @pl.when((q == 0) & (p > 0))
        def _():
            low.start()

        @pl.when((q == 1) & (p < pairs - 1))
        def _():
            high.start()

    for ch in range(chunks):
        xh.append(remote(hist_ref.at[:, cols(1 - q, ch)], hist_buf.at[q, ch],
                         xh_send.at[ch], xh_recv.at[ch], {"hist": partner}))
    xg = remote(gate_ref.at[:, gate_other], gate_buf.at[q], xg_send, xg_recv, {"hist": partner})
    queue = [(copy,) for copy in xt] + [(copy,) for copy in xh]
    queue[len(xt) + 1] += (xg,)

    def advance(i):
        if i < len(queue):
            for copy in queue[i]:
                copy.start()

    for i in range(WINDOW):
        advance(i)
    for r in range(pairs - 2):
        greet_line(ready_sem.at[r])
        pl.semaphore_wait(ready_sem.at[r], beside)

    for j in range(chunks // 2):
        xt[j].wait_recv()
        advance(j + WINDOW)
        xf[j].start()

    loads[0].wait()
    loads[1].wait()

    rs, up, down, ay = {}, {}, {}, {}

    def compute(ch):
        for copy in own[ch]:
            copy.wait()
        if ch % 2 == 0:
            xf[ch // 2].wait_recv()


        @pl.when((q == 0) & (p < pairs - 1))
        def _():
            zt[ch][0].wait_recv()

        @pl.when((q == 1) & (p > 0))
        def _():
            zt[ch][1].wait_recv()

        t0, t1 = taps_buf[0, ch], taps_buf[1, ch]
        first = fwd_buf[:, :rows]
        second = fwd_buf[:, rows:]
        s_a = dot(first, t0) + dot(second, t1)
        s_b = dot(first, t1)
        s_c = dot(second, taps_buf[2 - 2 * q, ch])
        xh[ch].wait_recv()
        advance(len(xt) + ch + WINDOW)
        h_a = dot(first, hist_buf[0, ch])
        h_b = dot(first, hist_buf[1, ch])
        h_c = dot(first, hist_buf[1 + q, ch])
        ra, ia = spectrum_product(s_a, h_a)
        rb, ib = spectrum_product(s_b, h_b)
        rc, ic = spectrum_product(s_c, h_c)
        conv = dot(inv_buf[:, :modes], (ra + rb + rc).astype(BF16)) + dot(
            inv_buf[:, modes:], (ia + ib + ic).astype(BF16)
        )
        conv = conv.reshape(pairs, conv.shape[0] // pairs, width)
        send_buf[ch] = conv.astype(BF16)
        own_buf[ch] = conv
        for d in range(1, pairs):
            to = (p + d) % pairs
            rs[ch, d] = remote(send_buf.at[ch, to], recv_buf.at[ch, d - 1],
                               rs_send.at[ch, d - 1], rs_recv.at[ch, d - 1],
                               {"hist": 2 * to + q})
            rs[ch, d].start()

    def reduce(ch):
        if ch == 0:
            loads[2].wait()
            xg.wait_recv()
        value = own_buf[ch, p]
        for d in range(1, pairs):
            rs[ch, d].wait_recv()
            value = value + recv_buf[ch, d - 1].astype(F32)
        gates = gate_buf[:, :, ch * width:(ch + 1) * width].astype(F32)
        gated = (value * gates.reshape(value.shape)).astype(BF16)
        gated_buf[ch, q, p] = gated
        line(ch, 0)

    def line(ch, s):
        if s > 0:
            left_slot = gated_buf.at[ch, q, (p - s + pairs) % pairs]
            right_slot = gated_buf.at[ch, q, (p + s) % pairs]
        else:
            left_slot = right_slot = gated_buf.at[ch, q, p]
        below = {"hist": jnp.maximum(me - 2, 0)}
        above = {"hist": jnp.minimum(me + 2, total - 1)}
        across = {"hist": partner}
        up[ch, s] = remote(left_slot, left_slot, az_send.at[ch, 0, s], az_recv.at[ch, 0, s], above)
        down[ch, s] = remote(right_slot, right_slot, az_send.at[ch, 1, s], az_recv.at[ch, 1, s], below)
        ay[ch, 0, s] = remote(left_slot, left_slot, ay_send.at[ch, 0, s], ay_recv.at[ch, 0, s], across)
        ay[ch, 1, s] = remote(right_slot, right_slot, ay_send.at[ch, 1, s], ay_recv.at[ch, 1, s], across)

        @pl.when(p - s >= 0)
        def _():
            if s > 0:
                up[ch, s - 1].wait_recv()

            @pl.when(p < pairs - 1)
            def _():
                up[ch, s].start()

            ay[ch, 0, s].start()

        @pl.when(p + s < pairs)
        def _():
            if s > 0:
                down[ch, s - 1].wait_recv()

            @pl.when(p > 0)
            def _():
                down[ch, s].start()

            if s > 0:
                ay[ch, 1, s].start()

    def project(ch):
        if ch == 0:
            loads[3].wait()
        ay[ch, 0, 0].wait_recv()
        for s in range(1, pairs):
            @pl.when(p - s >= 0)
            def _():
                ay[ch, 0, s].wait_recv()

            @pl.when(p + s < pairs)
            def _():
                ay[ch, 1, s].wait_recv()

        low = gated_buf[ch, 0].reshape(-1, width)
        high = gated_buf[ch, 1].reshape(-1, width)
        value = dot(low, weight_buf[ch * width:(ch + 1) * width]) + dot(
            high, weight_buf[half + ch * width:half + (ch + 1) * width]
        )
        value = value.reshape(acc_buf.shape)
        if ch == 0:
            acc_buf[...] = value
        else:
            acc_buf[...] += value

    events = []
    for ch in range(chunks):
        events.append((ch, 0, functools.partial(compute, ch)))
        events.append((ch + REDUCE_AT, 1, functools.partial(reduce, ch)))
        for s in range(1, pairs):
            events.append((ch + REDUCE_AT + s * LINE_STEP, 1 + s, functools.partial(line, ch, s)))
        events.append((ch + REDUCE_AT + pairs * LINE_STEP, 1 + pairs, functools.partial(project, ch)))
    for event in sorted(events, key=lambda entry: entry[:2]):
        event[2]()

    swap_send[...] = acc_buf[:, 1 - core].astype(BF16)
    swap = remote(swap_send, swap_recv, sw_send, sw_recv, {"chan": 1 - core})
    swap.start()
    swap.wait_recv()
    fin_buf[...] = (acc_buf[:, core] + swap_recv[...].astype(F32)).astype(BF16)
    fin = []
    for d in range(1, total):
        to = (me + d) % total
        fin.append(remote(fin_buf.at[to], res_buf.at[me], fin_send.at[d - 1], fin_recv.at[d - 1],
                          {"hist": to}))
        fin[-1].start()
    res_buf[me] = fin_buf[me]

    for ch in range(chunks):
        xh[ch].wait_send()
    for j in range(chunks // 2):
        xt[j].wait_send()
        xf[j].wait_send()
    for ch in range(chunks):
        @pl.when((q == 0) & (p > 0))
        def _():
            zt[ch][0].wait_send()

        @pl.when((q == 1) & (p < pairs - 1))
        def _():
            zt[ch][1].wait_send()

    xg.wait_send()
    for copy in rs.values():
        copy.wait_send()
    for ch in range(chunks):
        ay[ch, 0, 0].wait_send()
        for s in range(pairs):
            @pl.when(p - s >= 0)
            def _():
                if s > 0:
                    ay[ch, 0, s].wait_send()

                @pl.when(p < pairs - 1)
                def _():
                    up[ch, s].wait_send()

            @pl.when(p + s < pairs)
            def _():
                if s > 0:
                    ay[ch, 1, s].wait_send()

                @pl.when(p > 0)
                def _():
                    down[ch, s].wait_send()

    swap.wait_send()
    for copy in fin:
        copy.wait_recv()
    for k in range(total):
        out_ref[:, k * columns:(k + 1) * columns] = res_buf[k]
    for copy in fin:
        copy.wait_send()


def local_kernel(chunks, history, filter_taps, gate_values, out_weight):
    rows, channels = history.shape
    owned = gate_values.shape[0]
    total = lax.axis_size("hist")
    cores = lax.axis_size("chan")
    pairs = total // 2
    tokens = owned * total
    half = channels // 2
    width = half // chunks
    columns = out_weight.shape[1]
    part = owned // cores
    forward, inverse = tables(rows, tokens)
    modes2 = forward.shape[0]
    forward = jnp.asarray(forward, F32).astype(BF16)
    inverse = jnp.asarray(inverse, F32).astype(BF16)
    dma = pltpu.SemaphoreType.DMA
    others = pairs - 1
    scratch = [
        pltpu.VMEM((3, chunks, rows, width), BF16),
        pltpu.VMEM((3, chunks, rows, width), BF16),
        pltpu.VMEM((2, owned, half), BF16),
        pltpu.VMEM(out_weight.shape, BF16),
        pltpu.VMEM(forward.shape, BF16),
        pltpu.VMEM(inverse.shape, BF16),
        pltpu.VMEM((chunks, pairs, 2 * owned, width), BF16),
        pltpu.VMEM((chunks, pairs, 2 * owned, width), F32),
        pltpu.VMEM((chunks, others, 2 * owned, width), BF16),
        pltpu.VMEM((chunks, 2, pairs, 2 * owned, width), BF16),
        pltpu.VMEM((total, cores, part, columns), F32),
        pltpu.VMEM((total, part, columns), BF16),
        pltpu.VMEM((total, part, columns), BF16),
        pltpu.VMEM((total, part, columns), BF16),
        pltpu.VMEM((total, part, columns), BF16),
        dma((4,)), dma((2, chunks)),
        dma((chunks // 2,)), dma((chunks // 2,)), dma((chunks,)), dma((chunks,)), dma, dma,
        dma((chunks,)), dma((chunks,)), dma((chunks // 2,)), dma((chunks // 2,)),
        dma((chunks, others)), dma((chunks, others)),
        dma((chunks, 2, pairs)), dma((chunks, 2, pairs)),
        dma((chunks, 2, pairs)), dma((chunks, 2, pairs)),
        dma, dma, dma((total - 1,)), dma((total - 1,)),
        pltpu.SemaphoreType.REGULAR((pairs - 2,)),
    ]
    return pl.pallas_call(
        functools.partial(kernel, pairs, chunks),
        out_shape=jax.ShapeDtypeStruct((part, total * columns), BF16),
        in_specs=[pl.BlockSpec(memory_space=pl.ANY)] * 6,
        out_specs=pl.BlockSpec(memory_space=pltpu.VMEM),
        scratch_shapes=scratch,
        compiler_params=pltpu.CompilerParams(
            collective_id=0, has_side_effects=True, vmem_limit_bytes=67043328
        ),
    )(history, filter_taps, gate_values, out_weight, forward, inverse)


def local(history, filter_taps, gate_values, out_weight):
    rows, channels = history.shape
    owned = gate_values.shape[0]
    total = lax.axis_size("hist")
    cores = lax.axis_size("chan")
    fits = (
        total % 2 == 0
        and total >= 6
        and cores == 2
        and lax.axis_size("seq") == 2
        and CHUNKS % 2 == 0
        and owned % (16 * cores) == 0
        and rows == owned * total
        and channels % (128 * CHUNKS) == 0
        and out_weight.shape[1] % 128 == 0
    )
    if fits:
        return local_kernel(CHUNKS, history, filter_taps, gate_values, out_weight)
    return local_general(history, filter_taps, gate_values, out_weight)


def solution(mesh):
    return jax.shard_map(
        local,
        mesh=mesh,
        in_specs=(
            P(("seq", "hist"), "chan"),
            P("hist", "chan"),
            P(("seq", "hist"), "chan"),
            P("chan", "hist"),
        ),
        out_specs=P(("seq", "hist", "chan"), None),
        check_vma=False,
    )
```
